32 devices in a mesh: seq: 4 (over y, core), vocab: 8 (over z, x).
Axes of the slice: x: 2, y: 2, z: 4, core: 2. Of those that a mesh axis runs over, the one named last changes fastest.
Arguments:
- hidden: bfloat16 [2, 512, 5120], P(None, 'seq'), may hold values from -128 to 128
- head_weight: bfloat16 [5120, 77824], P('seq', 'vocab'), may hold values from -1 to 1
- ref_logits: bfloat16 [2, 512, 77824], P(None, 'seq', 'vocab'), may hold values from -320 to 320
- token_ids: int32 [2, 512], P(None, 'seq'), may hold values from 0 to 77823
- end_pos: int32 [2], replicated, may hold values from 256 to 511
- loss_mask: int32 [2, 512], P(None, 'seq'), may hold values 0 or 1
- scores: float32 [2], replicated, may hold values from -8 to 8
Outputs:
- logit_grad: bfloat16 [2, 512, 77824], P(None, 'seq', 'vocab')
- hidden_grad: bfloat16 [2, 512, 5120], P(None, 'seq', 'vocab')
- advantages: float32 [2, 512], P(None, 'seq')
The draws below stay inside these ranges and needn't reach their ends.
All inputs are finite; a program needn't handle non-finite values. No bound on the sum of `loss_mask` on one device may be relied on, other than what follows from the above.
Results may differ from the reference program's by a relative error of at most 0.0039.
The reference program's roundings to bfloat16 on the way count: a program that leaves them out, or rounds other values in their place, can miss the bound.
Values may be sent and summed in bfloat16 or wider, within the bound.
A program may use at most 128 MiB of HBM per device.

```python
import math
import jax
import jax.numpy as jnp
from jax import lax

D = 5120
VOCAB = 77824
BATCH = 2
SEQ_LEN = 512


HIDDEN_LIMIT = 128.0


def special_columns(key):
    base = jax.random.fold_in(key, 77)
    keys = jax.random.split(base, 4)
    first_index = jax.random.randint(keys[0], (), 0, VOCAB)
    second_index = (first_index + 1 + jax.random.randint(keys[1], (), 0, VOCAB - 1)) % VOCAB
    first_col = jax.random.normal(keys[2], (D,), jnp.float32) / math.sqrt(D)
    second_col = jax.random.normal(keys[3], (D,), jnp.float32) / math.sqrt(D)
    second_col = second_col - jnp.dot(second_col, first_col) / jnp.dot(first_col, first_col) * first_col
    return (first_index, second_index, first_col, second_col)


def head_column(key, column_index, specials):
    first_index, second_index, first_col, second_col = specials
    column = jax.random.normal(jax.random.fold_in(jax.random.fold_in(key, 5), column_index), (D,), jnp.float32)
    column = jnp.clip(column, -6.0, 6.0) / math.sqrt(D)
    column = jnp.where(column_index == first_index, first_col, column)
    return jnp.where(column_index == second_index, second_col, column)


def token_draw(key):
    return jax.random.randint(jax.random.fold_in(key, 31), (BATCH, SEQ_LEN), 0, VOCAB).astype(jnp.int32)


def draw_token_ids(key, part):
    return token_draw(key)


def draw_head_weight(key, part):
    specials = special_columns(key)
    columns = jax.vmap(lambda column_index: head_column(key, column_index, specials))(jnp.arange(VOCAB).astype(jnp.int32))
    return jnp.transpose(columns).astype(jnp.bfloat16)


def draw_hidden(key, part):
    states = 3.0 * jnp.clip(jax.random.normal(jax.random.fold_in(key, 6), (BATCH, SEQ_LEN, D), jnp.float32), -6.0, 6.0)
    specials = special_columns(key)
    tokens = token_draw(key).reshape(BATCH * SEQ_LEN)
    token_columns = jax.vmap(lambda column_index: head_column(key, column_index, specials))(tokens)
    token_columns = token_columns.reshape(BATCH, SEQ_LEN, D)
    boost_size = jax.random.uniform(jax.random.fold_in(key, 10), (BATCH, SEQ_LEN, 1), jnp.float32, 6.0, 19.0)
    states = states + boost_size * token_columns / jnp.sum(token_columns * token_columns, axis=2, keepdims=True)
    states = jnp.clip(states, -HIDDEN_LIMIT, HIDDEN_LIMIT)
    return states.astype(jnp.bfloat16)


def draw_ref_logits(key, part):
    values = 1.5 * jnp.clip(jax.random.normal(jax.random.fold_in(key, 21), (BATCH, SEQ_LEN, VOCAB), jnp.float32), -6.0, 6.0)
    return values.astype(jnp.bfloat16)


def with_ends(values, stream_key, low, top_value):
    shape = values.shape
    spot = [jax.random.randint(jax.random.fold_in(stream_key, axis), (), 0, shape[axis]) for axis in range(len(shape))]
    values = values.at[tuple(spot)].set(low)
    longest = shape.index(max(shape))
    spot[longest] = (spot[longest] + 1) % shape[longest]
    return values.at[tuple(spot)].set(top_value)


def centred(own_key, extent, scale, bound, held_as=jnp.bfloat16):
    result = scale * jax.random.normal(own_key, extent, jnp.float32)
    return jnp.clip(result, min=-bound, max=bound).astype(held_as)


def setup_inputs(seed: int = 0) -> dict:
    splits = jax.random.split(jax.random.key(seed), 8)
    return {
        "hidden": draw_hidden(jax.random.fold_in(splits[7], 71), 0),
        "head_weight": draw_head_weight(jax.random.fold_in(splits[7], 71), 0),
        "ref_logits": draw_ref_logits(jax.random.fold_in(splits[7], 71), 0),
        "token_ids": draw_token_ids(jax.random.fold_in(splits[7], 71), 0),
        "end_pos": jax.random.randint(splits[4], (BATCH,), SEQ_LEN // 2, SEQ_LEN).astype(jnp.int32),
        "loss_mask": with_ends((jax.random.randint(splits[5], (BATCH, SEQ_LEN), 0, 4) < 3).astype(jnp.int32), jax.random.fold_in(splits[5], 1), 0, 1),
        "scores": centred(splits[6], (BATCH,), 2.0, 8.0, jnp.float32),
    }


def row_stats(pair, head_weight):
    states, refs = pair
    logits = jnp.dot(states, head_weight, preferred_element_type=jnp.float32)
    refs = refs.astype(jnp.float32)
    top_policy = lax.optimization_barrier(jnp.max(logits, axis=1))
    expo = jnp.exp(logits - top_policy[:, None])
    total = lax.optimization_barrier(jnp.sum(expo, axis=1))
    weighted = lax.optimization_barrier(jnp.sum(expo * (logits - refs), axis=1))
    top_ref = lax.optimization_barrier(jnp.max(refs, axis=1))
    ref_total = lax.optimization_barrier(jnp.sum(jnp.exp(refs - top_ref[:, None]), axis=1))
    lse_policy = top_policy + jnp.log(total)
    lse_ref = top_ref + jnp.log(ref_total)
    return weighted / total - lse_policy + lse_ref

def grad_rows(triple, head_weight):
    states, tokens, factor = triple
    logits = jnp.dot(states, head_weight, preferred_element_type=jnp.float32)
    top_policy = lax.optimization_barrier(jnp.max(logits, axis=1))
    lse_policy = top_policy + jnp.log(lax.optimization_barrier(jnp.sum(jnp.exp(logits - top_policy[:, None]), axis=1)))
    prob = jnp.exp(logits - lse_policy[:, None])
    column = jnp.arange(logits.shape[1]).astype(jnp.int32)
    onehot = (column[None, :] == tokens[:, None]).astype(jnp.float32)
    grad = (factor[:, None] * (prob - onehot)).astype(jnp.bfloat16)
    back = jnp.dot(grad, head_weight.T, preferred_element_type=jnp.float32).astype(jnp.bfloat16)
    return (grad, back)

def reference(hidden, head_weight, ref_logits, token_ids, end_pos, loss_mask, scores):
    kl_value = lax.map(lambda pair: row_stats(pair, head_weight), (hidden, ref_logits))
    position = jnp.arange(SEQ_LEN).astype(jnp.int32)
    live = ((loss_mask == 1) & (position[None, :] <= end_pos[:, None])).astype(jnp.float32)
    at_end = (position[None, :] == end_pos[:, None]).astype(jnp.float32)
    reward = -0.01 * kl_value * live + scores[:, None] * at_end
    returns = jnp.cumsum(reward[:, ::-1], axis=1)[:, ::-1]
    count = jnp.maximum(jnp.sum(live), 1.0)
    mean = jnp.sum(live * returns) / count
    var = jnp.sum(live * returns * returns) / count - mean * mean
    advantages = (returns - mean) / jnp.sqrt(var + 1e-05)
    factor = live * advantages / count
    logit_grad, hidden_grad = lax.map(lambda triple: grad_rows(triple, head_weight), (hidden, token_ids, factor))
    return (logit_grad, hidden_grad, advantages)
```

```python
import functools

import jax
import jax.numpy as jnp
from jax import lax
from jax.experimental import pallas as pl
from jax.experimental.pallas import tpu as pltpu
from jax.sharding import PartitionSpec as P


CORES = 2
FORWARD_CHUNKS = 8
BACKWARD_CHUNKS = 2


def pieces(extent, parts, unit=128):
    blocks = extent // unit
    edges = [unit * (blocks * i // parts) for i in range(parts)] + [extent]
    return [(lo, hi) for lo, hi in zip(edges[:-1], edges[1:]) if hi > lo]


def exchange_kernel(axis, n, x_ref, out_ref, send_sem, recv_sem, local_sem):
    me = lax.axis_index(axis)
    barrier = pltpu.get_barrier_semaphore()
    for k in range(1, n):
        pl.semaphore_signal(
            barrier,
            inc=1,
            device_id={axis: lax.rem(me + k, n)},
            device_id_type=pl.DeviceIdType.MESH,
        )
    own = pltpu.make_async_copy(x_ref, out_ref.at[me], local_sem)
    own.start()
    pl.semaphore_wait(barrier, n - 1)
    copies = []
    for k in range(1, n):
        copy = pltpu.make_async_remote_copy(
            src_ref=x_ref,
            dst_ref=out_ref.at[me],
            send_sem=send_sem.at[k],
            recv_sem=recv_sem.at[k],
            device_id={axis: lax.rem(me + k, n)},
            device_id_type=pl.DeviceIdType.MESH,
        )
        copy.start()
        copies.append(copy)
    own.wait()
    for copy in copies:
        copy.wait()


def exchange(x, axis, collective_id):
    n = lax.axis_size(axis)
    return pl.pallas_call(
        functools.partial(exchange_kernel, axis, n),
        out_shape=jax.ShapeDtypeStruct((n,) + x.shape, x.dtype),
        in_specs=[pl.BlockSpec(memory_space=pltpu.VMEM)],
        out_specs=pl.BlockSpec(memory_space=pltpu.VMEM),
        scratch_shapes=[
            pltpu.SemaphoreType.DMA((n,)),
            pltpu.SemaphoreType.DMA((n,)),
            pltpu.SemaphoreType.DMA,
        ],
        compiler_params=pltpu.CompilerParams(
            collective_id=collective_id, has_side_effects=True
        ),
    )(x)


def rows_of(stack, rows):
    flat = jnp.concatenate(stack, axis=0)
    return jnp.pad(flat, ((0, rows - flat.shape[0]), (0, 0)))


def per_device(hidden, head_weight, ref_logits, token_ids, end_pos, loss_mask, scores):
    batch, segment, width = hidden.shape
    rows, vocab_dev = head_weight.shape
    seq_size = lax.axis_size("seq")
    vocab_size = lax.axis_size("vocab")
    chips = seq_size // CORES
    seq = lax.axis_index("seq")
    vocab = lax.axis_index("vocab")
    chip, core = seq // CORES, seq % CORES
    vocab_start = vocab * vocab_dev

    def sibling(x):
        return lax.ppermute(x, "seq", [(s, s ^ 1) for s in range(seq_size)])

    def shift(x, by):
        pairs = [(s, (s + CORES * by) % seq_size) for s in range(seq_size)]
        return lax.ppermute(x, "seq", pairs)

    def features(owner):
        mine = lax.dynamic_slice_in_dim(hidden, owner * rows, rows, axis=2)
        other = lax.dynamic_slice_in_dim(hidden, (owner ^ 1) * rows, rows, axis=2)
        return jnp.concatenate([mine, other], axis=2)

    chunks = pieces(vocab_dev, FORWARD_CHUNKS)
    states = [features(seq)]
    for r in range(1, chips):
        states.append(shift(features((seq - CORES * r) % seq_size), -r))
    weights = [head_weight[:, lo:hi] for lo, hi in chunks]
    weights = [(w, sibling(w)) for w in weights]

    def project(x, pair):
        mine, other = pair
        dot = functools.partial(
            jnp.einsum, "bsd,dv->bsv", preferred_element_type=jnp.float32
        )
        return dot(x[:, :, :rows], mine) + dot(x[:, :, rows:], other)

    logits, tops, totals, weighteds = [], [], [], []
    for (lo, hi), pair in zip(chunks, weights):
        sent = [shift(project(states[r], pair), r) for r in range(1, chips)]
        part = project(states[0], pair)
        for other in sent:
            part = part + other
        logits.append(part)
        top = jnp.max(part, axis=2)
        expo = jnp.exp(part - top[:, :, None])
        refs = ref_logits[:, :, lo:hi].astype(jnp.float32)
        tops.append(top)
        totals.append(jnp.sum(expo, axis=2))
        weighteds.append(jnp.sum(expo * (part - refs), axis=2))
    refs = ref_logits.astype(jnp.float32)
    local_rtop = jnp.max(refs, axis=2)
    local_rtotal = jnp.sum(jnp.exp(refs - local_rtop[:, :, None]), axis=2)

    def merge(top_list, sums_list):
        top = functools.reduce(jnp.maximum, top_list)
        scales = [jnp.exp(t - top) for t in top_list]
        return top, [
            functools.reduce(jnp.add, [s * x for s, x in zip(scales, sums)])
            for sums in sums_list
        ]

    local_top, (local_total, local_weighted) = merge(tops, (totals, weighteds))
    stats = exchange(
        rows_of((local_top, local_total, local_weighted, local_rtop, local_rtotal), 16),
        "vocab",
        0,
    )
    stats = [
        [stats[d, batch * i : batch * (i + 1)] for d in range(vocab_size)] for i in range(5)
    ]
    top_policy, (total, weighted) = merge(stats[0], (stats[1], stats[2]))
    top_ref, (ref_total,) = merge(stats[3], (stats[4],))
    lse_policy = top_policy + jnp.log(total)
    lse_ref = top_ref + jnp.log(ref_total)
    kl_value = weighted / total - lse_policy + lse_ref
    position = seq * segment + lax.broadcasted_iota(jnp.int32, (1, segment), 1)
    live = ((loss_mask == 1) & (position <= end_pos[:, None])).astype(jnp.float32)
    at_end = (position == end_pos[:, None]).astype(jnp.float32)
    reward = -0.01 * kl_value * live + scores[:, None] * at_end
    everyone = exchange(rows_of((reward, live), 8), "seq", 1)
    all_reward = everyone[:, :batch]
    all_live = everyone[:, batch : 2 * batch]
    upper = (
        lax.broadcasted_iota(jnp.int32, (segment, segment), 0)
        >= lax.broadcasted_iota(jnp.int32, (segment, segment), 1)
    ).astype(jnp.float32)
    returns = jnp.einsum("nbs,st->nbt", all_reward, upper, precision=lax.Precision.HIGHEST)
    block_totals = jnp.sum(all_reward, axis=2)
    carried = [jnp.zeros_like(block_totals[0])]
    for s in range(seq_size - 1, 0, -1):
        carried.append(carried[-1] + block_totals[s])
    returns = returns + jnp.stack(carried[::-1])[:, :, None]
    count = jnp.maximum(jnp.sum(all_live), 1.0)
    mean = jnp.sum(all_live * returns) / count
    var = jnp.sum(all_live * returns * returns) / count - mean * mean
    mine = lax.dynamic_index_in_dim(returns, seq, 0, keepdims=False)
    advantages = (mine - mean) / jnp.sqrt(var + 1e-05)
    factor = live * advantages / count

    grads = []
    for (lo, hi), part in zip(chunks, logits):
        prob = jnp.exp(part - lse_policy[:, :, None])
        column = vocab_start + lo + lax.broadcasted_iota(jnp.int32, (1, 1, hi - lo), 2)
        onehot = (column == token_ids[:, :, None]).astype(jnp.float32)
        grads.append((factor[:, :, None] * (prob - onehot)).astype(jnp.bfloat16))
    logit_grad = jnp.concatenate(grads, axis=2)

    blocks = vocab_size // chips
    block = width // vocab_size
    part_len = segment // chips

    def back(terms):
        halves = []
        for side in range(CORES):
            dots = [
                jnp.einsum("bsv,dv->bsd", g, pair[side], preferred_element_type=jnp.float32)
                for g, pair in terms
            ]
            halves.append(functools.reduce(jnp.add, dots))
        first = jnp.where(core == 0, halves[0], halves[1])
        second = jnp.where(core == 0, halves[1], halves[0])
        return jnp.concatenate([first, second], axis=2)

    def reduce_vocab(grad):
        n = grad.shape[0]
        split = grad.reshape(n, chips, part_len, blocks, block)
        split = jnp.transpose(split, (3, 1, 0, 2, 4)).reshape(
            vocab_size, n * part_len, block
        )
        summed = lax.psum_scatter(split, "vocab", scatter_dimension=0, tiled=False)
        return summed.reshape(n, part_len, block)

    groups = pieces(len(chunks), BACKWARD_CHUNKS, 1)
    sent = []
    for b in range(batch):
        for r in range(1, chips):
            for first, last in groups:
                g = jnp.concatenate([x[b : b + 1] for x in grads[first:last]], axis=2)
                sent.append(shift(g, -r))
    owned = [reduce_vocab(back(list(zip(grads, weights))))]
    others = [[] for _ in range(1, chips)]
    place = 0
    for b in range(batch):
        for r in range(1, chips):
            terms = []
            for first, last in groups:
                g = sent[place]
                place += 1
                base = chunks[first][0]
                for (lo, hi), pair in zip(chunks[first:last], weights[first:last]):
                    terms.append((g[:, :, lo - base : hi - base], pair))
            others[r - 1].append(reduce_vocab(back(terms)))
    owned += [jnp.concatenate(parts, axis=0) for parts in others]
    held = jnp.stack(owned).astype(jnp.bfloat16)

    mine_q = vocab % chips
    source = vocab // blocks
    hidden_grad = jnp.zeros((chips, batch, part_len, block), jnp.bfloat16)
    for k in range(chips):
        pairs = []
        for s in range(seq_size):
            for v in range(vocab_size):
                y, c = divmod(s, CORES)
                to = ((y + k - v % chips) % chips) * CORES + c
                pairs.append((s * vocab_size + v, to * vocab_size + blocks * y + v // chips))
        out = lax.dynamic_index_in_dim(held, (k - mine_q) % chips, 0, keepdims=False)
        got = lax.ppermute(out, ("seq", "vocab"), pairs)
        hidden_grad = lax.dynamic_update_index_in_dim(
            hidden_grad, got, (k - (chip - source)) % chips, 0
        )
    hidden_grad = jnp.transpose(hidden_grad, (1, 0, 2, 3)).reshape(batch, segment, block)
    return (logit_grad, hidden_grad, advantages)


def solution(mesh):
    in_specs = (
        P(None, "seq", None),
        P("seq", "vocab"),
        P(None, "seq", "vocab"),
        P(None, "seq"),
        P(),
        P(None, "seq"),
        P(),
    )
    out_specs = (P(None, "seq", "vocab"), P(None, "seq", "vocab"), P(None, "seq"))
    return jax.shard_map(
        per_device, mesh=mesh, in_specs=in_specs, out_specs=out_specs, check_vma=False
    )
```

```python
import functools

import jax
import jax.numpy as jnp
from jax import lax
from jax.experimental import pallas as pl
from jax.experimental.pallas import tpu as pltpu
from jax.sharding import PartitionSpec as P


CORES = 2
FORWARD_CHUNKS = 8
BACKWARD_CHUNKS = 8


def pieces(extent, parts, unit=128):
    blocks = extent // unit
    edges = [unit * (blocks * i // parts) for i in range(parts)] + [extent]
    return [(lo, hi) for lo, hi in zip(edges[:-1], edges[1:]) if hi > lo]


def exchange_kernel(axis, n, x_ref, out_ref, send_sem, recv_sem, local_sem):
    me = lax.axis_index(axis)
    barrier = pltpu.get_barrier_semaphore()
    for k in range(1, n):
        pl.semaphore_signal(
            barrier,
            inc=1,
            device_id={axis: lax.rem(me + k, n)},
            device_id_type=pl.DeviceIdType.MESH,
        )
    own = pltpu.make_async_copy(x_ref, out_ref.at[me], local_sem)
    own.start()
    pl.semaphore_wait(barrier, n - 1)
    copies = []
    for k in range(1, n):
        copy = pltpu.make_async_remote_copy(
            src_ref=x_ref,
            dst_ref=out_ref.at[me],
            send_sem=send_sem.at[k],
            recv_sem=recv_sem.at[k],
            device_id={axis: lax.rem(me + k, n)},
            device_id_type=pl.DeviceIdType.MESH,
        )
        copy.start()
        copies.append(copy)
    own.wait()
    for copy in copies:
        copy.wait()


def exchange(x, axis, collective_id):
    n = lax.axis_size(axis)
    return pl.pallas_call(
        functools.partial(exchange_kernel, axis, n),
        out_shape=jax.ShapeDtypeStruct((n,) + x.shape, x.dtype),
        in_specs=[pl.BlockSpec(memory_space=pltpu.VMEM)],
        out_specs=pl.BlockSpec(memory_space=pltpu.VMEM),
        scratch_shapes=[
            pltpu.SemaphoreType.DMA((n,)),
            pltpu.SemaphoreType.DMA((n,)),
            pltpu.SemaphoreType.DMA,
        ],
        compiler_params=pltpu.CompilerParams(
            collective_id=collective_id, has_side_effects=True
        ),
    )(x)


def rows_of(stack, rows):
    flat = jnp.concatenate(stack, axis=0)
    return jnp.pad(flat, ((0, rows - flat.shape[0]), (0, 0)))


def compute(hidden, head_weight, ref_logits, token_ids, end_pos, loss_mask, scores):
    batch, segment, width = hidden.shape
    rows, vocab_dev = head_weight.shape
    seq_size = lax.axis_size("seq")
    vocab_size = lax.axis_size("vocab")
    chips = seq_size // CORES
    seq = lax.axis_index("seq")
    vocab = lax.axis_index("vocab")
    chip, core = seq // CORES, seq % CORES
    vocab_start = vocab * vocab_dev

    def sibling(x):
        return lax.ppermute(x, "seq", [(s, s ^ 1) for s in range(seq_size)])

    def shift(x, by):
        pairs = [(s, (s + CORES * by) % seq_size) for s in range(seq_size)]
        return lax.ppermute(x, "seq", pairs)

    def features(owner):
        mine = lax.dynamic_slice_in_dim(hidden, owner * rows, rows, axis=2)
        other = lax.dynamic_slice_in_dim(hidden, (owner ^ 1) * rows, rows, axis=2)
        return jnp.concatenate([mine, other], axis=2)

    chunks = pieces(vocab_dev, FORWARD_CHUNKS)
    outgoing = [features((seq - CORES * r) % seq_size) for r in range(1, chips)]
    own_states = features(seq)
    states = [shift(x, -r) for r, x in enumerate(outgoing, 1)]
    swapped = lax.optimization_barrier((head_weight, *outgoing))[0]
    weights = [(head_weight[:, lo:hi], sibling(swapped[:, lo:hi])) for lo, hi in chunks]

    def project(x, pair):
        mine, other = pair
        dot = functools.partial(
            jnp.einsum, "bsd,dv->bsv", preferred_element_type=jnp.float32
        )
        return dot(x[:, :, :rows], mine) + dot(x[:, :, rows:], other)

    partials = [[project(x, pair) for x in states] for pair in weights]
    sent = [[shift(x, r) for r, x in enumerate(xs, 1)] for xs in partials]
    logits, tops, totals, weighteds = [], [], [], []
    for j, ((lo, hi), pair) in enumerate(zip(chunks, weights)):
        after = partials[min(j + 2, len(chunks) - 1)]
        part = project(lax.optimization_barrier((own_states, *after))[0], pair)
        for other in sent[j]:
            part = part + other
        logits.append(part)
        top = jnp.max(part, axis=2)
        expo = jnp.exp(part - top[:, :, None])
        refs = ref_logits[:, :, lo:hi].astype(jnp.float32)
        tops.append(top)
        totals.append(jnp.sum(expo, axis=2))
        weighteds.append(jnp.sum(expo * (part - refs), axis=2))
    refs = ref_logits.astype(jnp.float32)
    local_rtop = jnp.max(refs, axis=2)
    local_rtotal = jnp.sum(jnp.exp(refs - local_rtop[:, :, None]), axis=2)

    def merge(top_list, sums_list):
        top = functools.reduce(jnp.maximum, top_list)
        scales = [jnp.exp(t - top) for t in top_list]
        return top, [
            functools.reduce(jnp.add, [s * x for s, x in zip(scales, sums)])
            for sums in sums_list
        ]

    local_top, (local_total, local_weighted) = merge(tops, (totals, weighteds))
    stats = exchange(
        rows_of((local_top, local_total, local_weighted, local_rtop, local_rtotal), 16),
        "vocab",
        0,
    )
    stats = [
        [stats[d, batch * i : batch * (i + 1)] for d in range(vocab_size)] for i in range(5)
    ]
    top_policy, (total, weighted) = merge(stats[0], (stats[1], stats[2]))
    top_ref, (ref_total,) = merge(stats[3], (stats[4],))
    lse_policy = top_policy + jnp.log(total)
    lse_ref = top_ref + jnp.log(ref_total)
    kl_value = weighted / total - lse_policy + lse_ref
    position = seq * segment + lax.broadcasted_iota(jnp.int32, (1, segment), 1)
    live = ((loss_mask == 1) & (position <= end_pos[:, None])).astype(jnp.float32)
    at_end = (position == end_pos[:, None]).astype(jnp.float32)
    reward = -0.01 * kl_value * live + scores[:, None] * at_end
    everyone = exchange(rows_of((reward, live), 8), "seq", 1)
    all_reward = everyone[:, :batch]
    all_live = everyone[:, batch : 2 * batch]
    upper = (
        lax.broadcasted_iota(jnp.int32, (segment, segment), 0)
        >= lax.broadcasted_iota(jnp.int32, (segment, segment), 1)
    ).astype(jnp.float32)
    returns = jnp.einsum("nbs,st->nbt", all_reward, upper, precision=lax.Precision.HIGHEST)
    block_totals = jnp.sum(all_reward, axis=2)
    carried = [jnp.zeros_like(block_totals[0])]
    for s in range(seq_size - 1, 0, -1):
        carried.append(carried[-1] + block_totals[s])
    returns = returns + jnp.stack(carried[::-1])[:, :, None]
    count = jnp.maximum(jnp.sum(all_live), 1.0)
    mean = jnp.sum(all_live * returns) / count
    var = jnp.sum(all_live * returns * returns) / count - mean * mean
    mine = lax.dynamic_index_in_dim(returns, seq, 0, keepdims=False)
    advantages = (mine - mean) / jnp.sqrt(var + 1e-05)
    factor = live * advantages / count

    grads = []
    for (lo, hi), part in zip(chunks, logits):
        prob = jnp.exp(part - lse_policy[:, :, None])
        column = vocab_start + lo + lax.broadcasted_iota(jnp.int32, (1, 1, hi - lo), 2)
        onehot = (column == token_ids[:, :, None]).astype(jnp.float32)
        grads.append((factor[:, :, None] * (prob - onehot)).astype(jnp.bfloat16))
    logit_grad = jnp.concatenate(grads, axis=2)

    blocks = vocab_size // chips
    block = width // vocab_size
    part_rows = block // chips

    def back(terms):
        halves = []
        for g, pair in terms:
            g = lax.optimization_barrier((g, *halves))[0]
            dots = [
                jnp.einsum("dv,tv->dt", w, g, preferred_element_type=jnp.float32)
                for w in pair
            ]
            halves = [h + d for h, d in zip(halves, dots)] if halves else dots
        return halves

    low_bits = [1 << i for i in range((vocab_size // CORES).bit_length() - 1)]
    top_bit = vocab_size // CORES

    def reduce_vocab(halves, turn):
        rest = jnp.concatenate(halves, axis=0)
        tokens = rest.shape[1]
        bits = low_bits[turn:] + low_bits[:turn]
        lengths = [2] * (len(low_bits) + 1)
        rest = rest.reshape(*lengths, part_rows, tokens)
        left = [top_bit] + low_bits[::-1]
        for bit in bits + [top_bit]:
            axis = left.index(bit)
            left.remove(bit)
            mine = (vocab // bit) % 2
            if bit == top_bit:
                mine = mine ^ core
            keep = lax.dynamic_index_in_dim(rest, mine, axis, keepdims=False)
            give = lax.dynamic_index_in_dim(rest, 1 - mine, axis, keepdims=False)
            rest = keep + lax.ppermute(
                give, "vocab", [(v, v ^ bit) for v in range(vocab_size)]
            )
        return rest

    def reduce_all(halves):
        return [
            reduce_vocab([h[:, b * segment : (b + 1) * segment] for h in halves], b % 2)
            for b in range(batch)
        ]

    flat = [x.reshape(batch * segment, -1) for x in grads]
    groups = pieces(len(chunks), BACKWARD_CHUNKS, 1)
    packed = [jnp.concatenate(flat[first:last], axis=1) for first, last in groups]
    sent = [[shift(g, -r) for g in packed] for r in range(1, chips)]

    def terms_of(pieces_in):
        terms = []
        for g, (first, last) in zip(pieces_in, groups):
            base = chunks[first][0]
            for (lo, hi), pair in zip(chunks[first:last], weights[first:last]):
                terms.append((g[:, lo - base : hi - base], pair))
        return terms

    latest = back(terms_of(lax.optimization_barrier(packed)))
    owned = [reduce_all(latest)]
    for arrived in sent:
        arrived = [lax.optimization_barrier((g, *latest))[0] for g in arrived]
        latest = back(terms_of(arrived))
        owned.append(reduce_all(latest))
    held = jnp.stack([jnp.stack(parts, axis=1) for parts in owned]).astype(jnp.bfloat16)

    mine_q = vocab % chips
    source = vocab // blocks
    hidden_grad = jnp.zeros((chips, part_rows, batch, segment), jnp.bfloat16)
    for k in range(chips):
        pairs = []
        for s in range(seq_size):
            for v in range(vocab_size):
                y, c = divmod(s, CORES)
                to = ((y + k - v % chips) % chips) * CORES + c
                pairs.append((s * vocab_size + v, to * vocab_size + blocks * y + v // chips))
        out = lax.dynamic_index_in_dim(held, (k - mine_q) % chips, 0, keepdims=False)
        got = lax.ppermute(out, ("seq", "vocab"), pairs)
        hidden_grad = lax.dynamic_update_index_in_dim(
            hidden_grad, got, (k - (chip - source)) % chips, 0
        )
    hidden_grad = jnp.transpose(hidden_grad.reshape(block, batch, segment), (1, 2, 0))
    return (logit_grad, hidden_grad, advantages)


def solution(mesh):
    in_specs = (
        P(None, "seq", None),
        P("seq", "vocab"),
        P(None, "seq", "vocab"),
        P(None, "seq"),
        P(),
        P(None, "seq"),
        P(),
    )
    out_specs = (P(None, "seq", "vocab"), P(None, "seq", "vocab"), P(None, "seq"))
    return jax.shard_map(
        compute, mesh=mesh, in_specs=in_specs, out_specs=out_specs, check_vma=False
    )
```
